768 devices in a mesh: ctx: 16 (over z_hi, x), grp: 48 (over z_lo, y, core).
Axes of the slice: x: 4, y: 8, z: 12 (z_hi: 4, z_lo: 3; z = z_hi * 3 + z_lo), core: 2. Of those that a mesh axis runs over, the one named last changes fastest.
Arguments:
- tokens: bfloat16 [4096, 6144], P('ctx', 'grp'), may hold values from -6 to 6
- frames: int32 [4096], replicated, may hold values from 0 to 31, never falling along the last dimension, each value on 1 to 512 neighbouring positions
- qkv_weight: bfloat16 [6144, 18432], P(None, 'grp'), may hold values from -0.15309311 to 0.15309311
- out_weight: bfloat16 [6144, 6144], P(None, 'grp'), may hold values from -0.078125 to 0.078125
- cond_weight: bfloat16 [6144, 1536], P('grp'), may hold values from -0.078125 to 0.078125
- cond_bias: float32 [1536], replicated, may hold values from -3 to 3
- in_weight: bfloat16 [16, 1536], replicated, may hold values from -1.5 to 1.5
- mid_weight: bfloat16 [1536, 1536], replicated, may hold values from -0.15625 to 0.15625
- noise_out_weight: bfloat16 [1536, 16], replicated, may hold values from -0.15625 to 0.15625
- head_gain: float32 [1536], replicated, may hold values from 0.5 to 1.5
- targets: float32 [4096, 16], P('ctx'), may hold values from -6 to 6
- noise_draws: float32 [4096, 64], P('ctx'), may hold values from -6 to 6
- timesteps: int32 [4096, 4], P('ctx'), may hold values from 0 to 999
- masked: int32 [4096], P('ctx'), may hold values 0 or 1
- routes: int32 [4096, 1], P('ctx'), may hold values from 0 to 47; in each aligned block of 256 rows (0 to 255, 256 to 511, ...) at most 8 rows name the same one
Outputs:
- hidden_state: bfloat16 [4096, 6144], P('ctx', 'grp')
- predicted_noise: float32 [6144, 64], P(('ctx', 'grp'))
The draws below stay inside these ranges and needn't reach their ends.
Inputs may be any that keep to these rules, and one draw needn't show every extreme that they name: `frames`: frame indices never fall along the clip; each frame has 1 to 512 tokens. `routes`: within the 256 tokens of one index of ctx, at most 8 tokens name any one value, a bound that some block reaches.
All inputs are finite; a program needn't handle non-finite values. No bound on the sum of `masked` on one device may be relied on, other than what follows from the above.
Results may differ from the reference program's by a relative error of at most 0.01.
The reference program's roundings to bfloat16 on the way (of `qkv`, `weights`, `attended`, `noisy`, `normed` and `block`) count: a program that leaves them out, or rounds other values in their place, can miss the bound.
Values may be sent and summed in bfloat16 or wider, within the bound.
No kernel may reach another device: no remote copies, remote signals or barrier semaphores. Data moves between devices by JAX's collectives and lax.ppermute only.
A program may use at most 64 MiB of HBM per device.

```python
import math
import jax
import jax.numpy as jnp
import numpy as np
from jax import lax

D = 6144
HD = 128
HEADS = 48
HW = 1536
LAT = 16
DRAWS = 4
TOK_DEV = 256
TOKENS = 4096
CAP = 8
SLOTS = 6144
FRAMES = 32
FRAME_MOST = 512
N_CTX = 16
N_GRP = 48


def draw_qkv_weight(key, part):
    key_entries = jax.random.fold_in(key, 11)
    key_heads = jax.random.fold_in(key, 12)
    entries = jnp.clip(jax.random.normal(key_entries, (D, HEADS, 3, HD), jnp.float32), -2.985, 2.985)
    head_level = jax.random.uniform(key_heads, (HEADS,), jnp.float32)
    head_factor = 4.0 ** head_level
    scaled_cols = jnp.array([1.0, 1.0, 0.0], jnp.float32)
    column_scale = 1.0 + (head_factor[:, None] - 1.0) * scaled_cols[None, :]
    weight = entries * column_scale[None, :, :, None] / math.sqrt(D)
    return weight.reshape(D, HEADS * 3 * HD).astype(jnp.bfloat16)


def place_ends(values, key, least, high):
    spot = [jax.random.randint(jax.random.fold_in(key, axis), (), 0, length) for axis, length in enumerate(values.shape)]
    main_axis = values.shape.index(max(values.shape))
    next_to = spot[:main_axis] + [(spot[main_axis] + 1) % values.shape[main_axis]] + spot[main_axis + 1:]
    return values.at[tuple(spot)].set(least).at[tuple(next_to)].set(high)


def block_scale(key, shape, cuts, smallest, top_value):
    factor_of, own = 1.0, jax.random.fold_in(key, 6)
    for dim, parts in cuts:
        draws = jnp.exp(jax.random.uniform(jax.random.fold_in(own, dim), (parts,), jnp.float32, smallest / len(cuts), top_value / len(cuts)))
        factor_of = factor_of * jnp.repeat(draws, shape[dim] // parts).reshape([-1 if axis == dim else 1 for axis in range(len(shape))])
    return factor_of


def length_profile(number_of, total, bound, slope):
    portions = [(1 << 20) // math.isqrt(standing ** slope) + 1 for standing in range(2, number_of + 1)]
    surplus, given = total - bound - (number_of - 1), [1] * (number_of - 1)
    while surplus > 0:
        free = [i for i in range(number_of - 1) if given[i] < bound]
        pool, remaining = sum([portions[i] for i in free]), surplus
        for i in free:
            extra = min(bound - given[i], max(1, remaining * portions[i] // pool), surplus)
            given[i] = given[i] + extra
            surplus = surplus - extra
    return np.array([bound] + given)


def ragged_sizes(rng, amount, total, most, slope):
    if amount == 2:
        one = jax.random.randint(rng, (), max(1, total - most), min(most, total - 1) + 1)
        return jnp.stack([one, total - one])
    sizes = jnp.asarray(length_profile(amount, total, most, slope), jnp.int32)
    pairs = (amount - 1) // 2
    source_of, sink = sizes[1:1 + 2 * pairs:2], sizes[2:2 + 2 * pairs:2]
    room = jnp.minimum(source_of - 1, most - sink)
    moved = jax.random.randint(jax.random.fold_in(rng, 1), (pairs,), 0, 1 << 20) % (room + 1)
    sizes = sizes.at[1:1 + 2 * pairs:2].set(source_of - moved).at[2:2 + 2 * pairs:2].set(sink + moved)
    return sizes[jax.random.permutation(jax.random.fold_in(rng, 2), amount)]


def routed_block(key, own, number, rows, count, top, most, lean):
    ranking = jax.random.permutation(key, count)
    packed, common = portions_of(count, rows * top, most, lean, True), portions_of(count, rows * top, most, lean, False)
    places = jnp.arange(count)

    def named(tallies, rotation):
        used = int((tallies > 0).sum())
        fixed = max(1, used // 4)
        passed = fixed + (places - fixed + rotation * (used - fixed)) % max(1, count - fixed)
        return jnp.zeros((count,), jnp.int32).at[ranking[jnp.where(places < fixed, places, passed)]].set(jnp.asarray(tallies, jnp.int32))

    tallies = jnp.where(number % 4 == 0, named(packed, number // 4), named(common, number - number // 4 - 1))
    mixed = jax.random.permutation(jax.random.fold_in(own, 3), count)
    source_of, sink = mixed[0:count // 2 * 2:2], mixed[1:count // 2 * 2:2]
    slack = jnp.minimum(tallies[source_of] - 1, most - tallies[sink]) // 2
    slack = jnp.where((source_of == ranking[0]) | (sink == ranking[0]) | (tallies[sink] == 0), 0, jnp.maximum(slack, 0))
    passed = jax.random.randint(jax.random.fold_in(own, 4), (count // 2,), 0, 1 << 20) % (slack + 1)
    tallies = tallies.at[source_of].add(-passed).at[sink].add(passed)
    items = jnp.searchsorted(jnp.cumsum(tallies), jnp.arange(rows * top), side="right").astype(jnp.int32)
    grid = items.reshape(top, rows).T
    grid = grid[jax.random.permutation(jax.random.fold_in(own, 1), rows)]
    rotation = jax.random.randint(jax.random.fold_in(own, 2), (rows, 1), 0, top)
    return jnp.take_along_axis(grid, (jnp.arange(top)[None, :] + rotation) % top, axis=1)


def portions_of(count, total, bound, skew, full):
    weights = [(1 << 20) // math.isqrt(grade ** skew) + 1 for grade in range(1, count + 1)]
    largest = bound if full else min(bound, max(-(-total // count), total * weights[0] // sum(weights)))
    least = 1 if total - largest >= count - 1 else 0
    counts, rest = [largest] + [least] * (count - 1), total - largest - least * (count - 1)
    while rest > 0:
        candidates = [i for i in range(1, count) if counts[i] < largest] or [i for i in range(1, count) if counts[i] < bound]
        whole, left = sum([weights[i] for i in candidates]), rest
        for i in candidates:
            addition = min(bound - counts[i], max(1, left * weights[i] // whole), rest)
            counts[i] = counts[i] + addition
            rest = rest - addition
    return np.array(counts)


def bell_draw(stream_key, shape, scale, bound, shards=(), kind=jnp.bfloat16):
    drawn = jax.random.normal(stream_key, shape, jnp.float32) * scale
    if len(shards) > 0:
        drawn = block_scale(stream_key, shape, shards, -0.22, 0.18) * drawn
    return jnp.clip(drawn, min=-bound, max=bound).astype(kind)


def setup_inputs(seed: int = 0) -> dict:
    seeds = jax.random.split(jax.random.key(seed), 16)
    tokens = bell_draw(seeds[0], (TOKENS, D), 1.0, 6.0, ((0, 16), (1, 48)))
    frames = jnp.searchsorted(jnp.cumsum(ragged_sizes(seeds[1], FRAMES, TOKENS, FRAME_MOST, 0)), jnp.arange(TOKENS), side="right").astype(jnp.int32)
    qkv_weight = draw_qkv_weight(jax.random.fold_in(seeds[15], 71), 0)
    out_weight = bell_draw(seeds[3], (HEADS * HD, D), (HEADS * HD) ** -0.5, 0.078125, ((1, 48),))
    cond_weight = bell_draw(seeds[4], (D, HW), D ** -0.5, 0.078125, ((0, 48),))
    cond_bias = bell_draw(seeds[5], (HW,), 0.5, 3.0, (), jnp.float32)
    in_weight = bell_draw(seeds[6], (LAT, HW), LAT ** -0.5, 1.5)
    mid_weight = bell_draw(seeds[7], (HW, HW), HW ** -0.5, 0.15625)
    noise_out_weight = bell_draw(seeds[8], (HW, LAT), HW ** -0.5, 0.15625)
    head_gain = jnp.clip(1.0 + 0.1 * jax.random.normal(seeds[9], (HW,), jnp.float32), 0.5, 1.5)
    targets = bell_draw(seeds[10], (TOKENS, LAT), 1.0, 6.0, ((0, 16),), jnp.float32)
    noise_draws = bell_draw(seeds[11], (TOKENS, DRAWS * LAT), 1.0, 6.0, ((0, 16),), jnp.float32)
    timesteps = place_ends(jax.random.randint(seeds[12], (TOKENS, DRAWS), 0, 1000), jax.random.fold_in(seeds[12], 1), 0, 999).astype(jnp.int32)
    masked = place_ends((jax.random.randint(seeds[13], (TOKENS,), 0, 4) < 3).astype(jnp.int32), jax.random.fold_in(seeds[13], 1), 0, 1)
    routes_keys = jax.random.split(jax.random.fold_in(seeds[14], 1), TOKENS // TOK_DEV)
    routes_turns = jax.random.permutation(jax.random.fold_in(seeds[14], 3), TOKENS // TOK_DEV)
    routes = jax.vmap(lambda own, number: routed_block(jax.random.fold_in(seeds[14], 2), own, number, TOK_DEV, N_GRP, 1, CAP, 2))(routes_keys, routes_turns).reshape((TOKENS, 1))
    return dict(tokens=tokens, frames=frames, qkv_weight=qkv_weight, out_weight=out_weight, cond_weight=cond_weight, cond_bias=cond_bias, in_weight=in_weight, mid_weight=mid_weight, noise_out_weight=noise_out_weight, head_gain=head_gain, targets=targets, noise_draws=noise_draws, timesteps=timesteps, masked=masked, routes=routes)


def alpha_bar(steps_float):
    return jnp.cos((steps_float / 1000.0 + 0.008) / 1.008 * (math.pi / 2)) ** 2

def time_embed(steps_float, width):
    half_width = width // 2
    freqs = jnp.exp(-math.log(10000.0) * jnp.arange(half_width, dtype=jnp.float32) / half_width)
    angles = steps_float[..., None] * freqs
    return jnp.concatenate([jnp.cos(angles), jnp.sin(angles)], axis=-1)

def head_rows(conditioning, target_rows, noise_rows, steps_float, in_weight, mid_weight, noise_out_weight, head_gain):
    count = conditioning.shape[0]
    latent = target_rows.shape[1]
    draws_count = steps_float.shape[1]
    width = in_weight.shape[1]
    abar = alpha_bar(steps_float)[..., None]
    noisy = jnp.sqrt(abar) * target_rows[:, None, :] + jnp.sqrt(1.0 - abar) * noise_rows.reshape(count, draws_count, latent)
    noisy = noisy.astype(jnp.bfloat16).reshape(count * draws_count, latent)
    lifted = jnp.dot(noisy, in_weight, preferred_element_type=jnp.float32).reshape(count, draws_count, width)
    lifted = lifted + conditioning[:, None, :] + time_embed(steps_float, width)
    scale = lax.rsqrt(lax.optimization_barrier(jnp.mean(lifted * lifted, axis=-1, keepdims=True)) + 1e-06)
    normed = (lifted * scale * head_gain).astype(jnp.bfloat16).reshape(count * draws_count, width)
    middle = jnp.dot(normed, mid_weight, preferred_element_type=jnp.float32)
    block = (lifted.reshape(count * draws_count, width) + jax.nn.silu(middle)).astype(jnp.bfloat16)
    result = jnp.dot(block, noise_out_weight, preferred_element_type=jnp.float32)
    return result.reshape(count, draws_count * latent)

def reference(tokens, frames, qkv_weight, out_weight, cond_weight, cond_bias, in_weight, mid_weight, noise_out_weight, head_gain, targets, noise_draws, timesteps, masked, routes):
    total_rows = tokens.shape[0]
    head_count = qkv_weight.shape[1] // (3 * HD)
    qkv = jnp.dot(tokens, qkv_weight, preferred_element_type=jnp.float32).astype(jnp.bfloat16)
    qkv = qkv.reshape(total_rows, head_count, 3, HD)
    allowed = frames[None, :] <= frames[:, None]

    def one_head(head_index):
        part = lax.dynamic_index_in_dim(qkv, head_index, 1, keepdims=False)
        queries = part[:, 0]
        keys_here = part[:, 1]
        values_here = part[:, 2]
        scores = jnp.dot(queries, keys_here.T, preferred_element_type=jnp.float32) * HD ** (-0.5)
        scores = jnp.where(allowed, scores, -1e+30)
        row_max = lax.optimization_barrier(jnp.max(scores, axis=1, keepdims=True))
        weights = jnp.where(allowed, jnp.exp(scores - row_max), 0.0)
        row_total = lax.optimization_barrier(jnp.sum(weights, axis=1, keepdims=True))
        summed = jnp.dot(weights.astype(jnp.bfloat16), values_here, preferred_element_type=jnp.float32)
        return (summed / row_total).astype(jnp.bfloat16)
    per_head = lax.map(one_head, jnp.arange(head_count, dtype=jnp.int32))
    attended = jnp.transpose(per_head, (1, 0, 2)).reshape(total_rows, head_count * HD)
    projected = jnp.dot(attended, out_weight, preferred_element_type=jnp.float32)
    hidden_state = (tokens.astype(jnp.float32) + projected).astype(jnp.bfloat16)
    conditioning = jnp.dot(hidden_state, cond_weight, preferred_element_type=jnp.float32) + cond_bias
    steps_float = timesteps.astype(jnp.float32)
    predictions = head_rows(conditioning, targets, noise_draws, steps_float, in_weight, mid_weight, noise_out_weight, head_gain)
    target_dev = routes[:, 0]
    onehot = (target_dev[:, None] == jnp.arange(N_GRP, dtype=jnp.int32)[None, :]).astype(jnp.int32) * masked[:, None]
    blocked = onehot.reshape(N_CTX, TOK_DEV, N_GRP)
    before = (jnp.cumsum(blocked, axis=1) - blocked).reshape(total_rows, N_GRP)
    slot_rank = lax.optimization_barrier(jnp.sum(before * onehot, axis=1))
    block_index = (jnp.arange(total_rows, dtype=jnp.int32) // TOK_DEV).astype(jnp.int32)
    slot_index = (block_index * N_GRP + target_dev) * CAP + slot_rank
    slot_index = jnp.where(masked == 1, slot_index, SLOTS).astype(jnp.int32)
    predicted_noise = jnp.zeros((SLOTS, predictions.shape[1]), jnp.float32).at[slot_index].set(predictions, mode='drop')
    return (hidden_state, predicted_noise)
```

```python
import math

import jax
import jax.numpy as jnp
from jax import lax
from jax.experimental import pallas as pl
from jax.experimental.pallas import tpu as pltpu
from jax.sharding import Mesh
from jax.sharding import PartitionSpec as P

CTX = ("zh", "x")
GRP = ("zl", "y", "core")
ALL = CTX + GRP
FRAME_VALUES = 32
BF16, F32 = jnp.bfloat16, jnp.float32


def copies_of(value, axes):
    tiles = jnp.broadcast_to(value[None], (lax.axis_size(axes), *value.shape))
    return lax.all_to_all(tiles, axes, split_axis=0, concat_axis=0, tiled=True)


def shifted(value, axis, by):
    n = lax.axis_size(axis)
    return lax.ppermute(value, axis, [(i, (i + by) % n) for i in range(n)])


def qkv_of(own, other, weight, core):
    chips, rows, feats = own.shape
    cols = weight.shape[1]
    head = cols // 3
    per = next(k for k in (4, 3, 2, 1) if chips % k == 0)
    weight = weight.reshape(chips, 2, feats, cols)

    def kernel(core_ref, own_ref, other_ref, wo_ref, wx_ref, q_ref, kv_ref, total):
        step = pl.program_id(0)

        @pl.when(step == 0)
        def _():
            total[...] = jnp.zeros_like(total)

        acc = total[...]
        for k in range(per):
            left = jnp.concatenate([own_ref[k], other_ref[k]], axis=1)
            right = jnp.concatenate([wo_ref[k, 0], wx_ref[k, 0]], axis=0)
            acc = acc + jnp.dot(left, right, preferred_element_type=F32)
        total[...] = acc

        @pl.when(step == pl.num_programs(0) - 1)
        def _():
            done = total[...].astype(BF16)
            q_ref[...] = done[:, :head]
            kv_ref[...] = done[:, head:]

    return pl.pallas_call(
        kernel,
        out_shape=(
            jax.ShapeDtypeStruct((rows, head), BF16),
            jax.ShapeDtypeStruct((rows, 2 * head), BF16),
        ),
        grid_spec=pltpu.PrefetchScalarGridSpec(
            num_scalar_prefetch=1,
            grid=(chips // per,),
            in_specs=[
                pl.BlockSpec((per, rows, feats), lambda i, c: (i, 0, 0)),
                pl.BlockSpec((per, rows, feats), lambda i, c: (i, 0, 0)),
                pl.BlockSpec((per, 1, feats, cols), lambda i, c: (i, c[0], 0, 0)),
                pl.BlockSpec((per, 1, feats, cols), lambda i, c: (i, 1 - c[0], 0, 0)),
            ],
            out_specs=[
                pl.BlockSpec((rows, head), lambda i, c: (0, 0)),
                pl.BlockSpec((rows, 2 * head), lambda i, c: (0, 0)),
            ],
            scratch_shapes=[pltpu.VMEM((rows, cols), F32)],
        ),
        name="qkv",
    )(core, own, other, weight, weight)


def partial_attention(queries, kvs, limits, starts):
    blocks, rows, head = queries.shape
    count = len(kvs)
    scale = head ** (-0.5)

    def kernel(starts_ref, limit_ref, q_ref, *refs):
        kv_refs, out_ref = refs[:count], refs[count]
        q = q_ref[0]
        limit = limit_ref[0]
        place = lax.broadcasted_iota(jnp.int32, (rows, rows), 0)
        scores, allowed = [], []
        top = jnp.full((1, rows), -1e30, F32)
        for k in range(count):
            s = lax.dot_general(
                kv_refs[k][:, :head], q, (((1,), (1,)), ((), ())), preferred_element_type=F32
            )
            ok = place < limit - starts_ref[k]
            s = jnp.where(ok, s * scale, -1e30)
            top = jnp.maximum(top, jnp.max(s, axis=0, keepdims=True))
            scores.append(s)
            allowed.append(ok)
        total = jnp.zeros((1, rows), F32)
        weighted = jnp.zeros((head, rows), F32)
        for k in range(count):
            w = jnp.where(allowed[k], jnp.exp(scores[k] - top), 0.0)
            total = total + jnp.sum(w, axis=0, keepdims=True)
            weighted = weighted + lax.dot_general(
                kv_refs[k][:, head:],
                w.astype(BF16),
                (((0,), (0,)), ((), ())),
                preferred_element_type=F32,
            )
        out_ref[0, :head, :] = weighted
        out_ref[0, head : head + 8, :] = jnp.where(
            lax.broadcasted_iota(jnp.int32, (8, rows), 0) == 0, top, total
        )

    return pl.pallas_call(
        kernel,
        out_shape=jax.ShapeDtypeStruct((blocks, head + 8, rows), F32),
        grid_spec=pltpu.PrefetchScalarGridSpec(
            num_scalar_prefetch=1,
            grid=(blocks,),
            in_specs=[
                pl.BlockSpec((1, 1, rows), lambda i, s: (i, 0, 0)),
                pl.BlockSpec((1, rows, head), lambda i, s: (i, 0, 0)),
            ]
            + [pl.BlockSpec((rows, 2 * head), lambda i, s: (0, 0))] * count,
            out_specs=pl.BlockSpec((1, head + 8, rows), lambda i, s: (i, 0, 0)),
        ),
        name="attention",
    )(starts, limits, queries, *kvs)


def merged_attention(parts):
    count, height, rows = parts.shape
    head = height - 8

    def kernel(parts_ref, out_ref):
        tops = [parts_ref[k, head : head + 1, :] for k in range(count)]
        top = tops[0]
        for k in range(1, count):
            top = jnp.maximum(top, tops[k])
        total = jnp.zeros((1, rows), F32)
        weighted = jnp.zeros((head, rows), F32)
        for k in range(count):
            factor = jnp.exp(tops[k] - top)
            total = total + factor * parts_ref[k, head + 1 : head + 2, :]
            weighted = weighted + factor * parts_ref[k, :head, :]
        out_ref[...] = (weighted / total).T.astype(BF16)

    return pl.pallas_call(
        kernel, out_shape=jax.ShapeDtypeStruct((rows, head), BF16), name="merge"
    )(parts)


def out_parts(attended, weight):
    n, rows, feats = attended.shape
    m, cols = weight.shape[0], weight.shape[3]

    def kernel(a_ref, w_ref, out_ref):
        left = jnp.concatenate([a_ref[k] for k in range(n)], axis=1)
        right = [w_ref[k].reshape(n * feats, cols) for k in range(2)]
        both = jnp.dot(left, jnp.concatenate(right, axis=1), preferred_element_type=F32)
        out_ref[0] = both[:, :cols].astype(BF16)
        out_ref[1] = both[:, cols:].astype(BF16)

    return pl.pallas_call(
        kernel,
        out_shape=jax.ShapeDtypeStruct((m, rows, cols), BF16),
        grid=(m // 2,),
        in_specs=[
            pl.BlockSpec((n, rows, feats), lambda i: (0, 0, 0)),
            pl.BlockSpec((2, n, feats, cols), lambda i: (i, 0, 0, 0)),
        ],
        out_specs=pl.BlockSpec((2, rows, cols), lambda i: (i, 0, 0)),
        name="out_parts",
    )(attended, weight)


def conditioning_parts(core, slot_of, own, other, weight_own, weight_other, chips, capacity):
    rows, feats = own.shape
    width = weight_own.shape[1]
    slots = chips * capacity

    def kernel(core_ref, slot_ref, own_ref, other_ref, wo_ref, wx_ref, out_ref):
        mine = lax.broadcasted_iota(jnp.int32, (slots, rows), 0)
        mine = mine + (mine // capacity) * capacity + core_ref[0] * capacity
        chooser = jnp.where(mine == slot_ref[...], 1.0, 0.0).astype(BF16)
        features = jnp.concatenate([own_ref[...], other_ref[...]], axis=1)
        picked = jnp.dot(chooser, features, preferred_element_type=F32).astype(BF16)
        weight = jnp.concatenate([wo_ref[...], wx_ref[...]], axis=0)
        out_ref[...] = jnp.dot(picked, weight, preferred_element_type=F32).astype(BF16)

    return pl.pallas_call(
        kernel,
        out_shape=jax.ShapeDtypeStruct((slots, width), BF16),
        in_specs=[pl.BlockSpec(memory_space=pltpu.SMEM)] + [pl.BlockSpec(memory_space=pltpu.VMEM)] * 5,
        name="cond_parts",
    )(core, slot_of, own, other, weight_own, weight_other)


def alpha_bar(steps_float):
    return jnp.cos((steps_float / 1000.0 + 0.008) / 1.008 * (math.pi / 2)) ** 2


def time_embed(steps_float, width):
    half_width = width // 2
    freqs = jnp.exp(-math.log(10000.0) * jnp.arange(half_width, dtype=F32) / half_width)
    angles = steps_float[..., None] * freqs
    return jnp.concatenate([jnp.cos(angles), jnp.sin(angles)], axis=-1)


def head_rows(
    conditioning,
    target_rows,
    noise_rows,
    steps_float,
    in_weight,
    mid_weight,
    noise_out_weight,
    head_gain,
):
    count = conditioning.shape[0]
    latent = target_rows.shape[1]
    draws_count = steps_float.shape[1]
    width = in_weight.shape[1]
    abar = alpha_bar(steps_float)[..., None]
    noisy = jnp.sqrt(abar) * target_rows[:, None, :] + jnp.sqrt(1.0 - abar) * noise_rows.reshape(
        count, draws_count, latent
    )
    noisy = noisy.astype(BF16).reshape(count * draws_count, latent)
    lifted = jnp.dot(noisy, in_weight, preferred_element_type=F32).reshape(
        count, draws_count, width
    )
    lifted = lifted + conditioning[:, None, :] + time_embed(steps_float, width)
    scale = lax.rsqrt(jnp.mean(lifted * lifted, axis=-1, keepdims=True) + 1e-06)
    normed = (lifted * scale * head_gain).astype(BF16).reshape(count * draws_count, width)
    middle = jnp.dot(normed, mid_weight, preferred_element_type=F32)
    block = (lifted.reshape(count * draws_count, width) + jax.nn.silu(middle)).astype(BF16)
    result = jnp.dot(block, noise_out_weight, preferred_element_type=F32)
    return result.reshape(count, draws_count * latent)


def shards(
    tokens,
    frames,
    qkv_weight,
    out_weight,
    cond_weight,
    cond_bias,
    in_weight,
    mid_weight,
    noise_out_weight,
    head_gain,
    targets,
    noise_draws,
    timesteps,
    masked,
    routes,
):
    rows, feats = tokens.shape
    zl, y = lax.axis_size("zl"), lax.axis_size("y")
    n_zh, n_x = lax.axis_size("zh"), lax.axis_size("x")
    chips = zl * y
    core = lax.axis_index("core")[None].astype(jnp.int32)

    own = copies_of(tokens, ("zl", "y"))
    other = shifted(own, "core", 1)
    queries, kv = qkv_of(own, other, qkv_weight, core)

    kvs = [kv] + [shifted(kv, "zh", by) for by in range(1, n_zh)]
    at = lax.axis_index("zh")
    starts = jnp.stack(
        [
            (((at - by) % n_zh) * n_x + lax.axis_index("x")) * rows
            for by in range(n_zh)
        ]
    ).astype(jnp.int32)
    below = jnp.sum(
        frames[None, :] <= jnp.arange(FRAME_VALUES, dtype=jnp.int32)[:, None], axis=1, dtype=jnp.int32
    )
    query_frames = lax.dynamic_slice_in_dim(frames, at * n_x * rows, n_x * rows)
    limits = jnp.sum(
        jnp.where(
            query_frames[None, :] == jnp.arange(FRAME_VALUES, dtype=jnp.int32)[:, None],
            below[:, None],
            0,
        ),
        axis=0,
    ).reshape(n_x, 1, rows)
    parts = partial_attention(copies_of(queries, "x"), kvs, limits, starts)
    attended = merged_attention(
        lax.all_to_all(parts, "x", split_axis=0, concat_axis=0, tiled=True)
    )

    weight_rows = out_weight.reshape(zl, y, 2, feats, feats).transpose(1, 0, 2, 3, 4)
    weight_rows = lax.all_to_all(
        weight_rows.reshape(y, zl * 2, feats, feats), "y", split_axis=0, concat_axis=0, tiled=True
    )
    sums = out_parts(copies_of(attended, ("zl", "core")), weight_rows)
    sums = lax.all_to_all(sums, "y", split_axis=0, concat_axis=0, tiled=True)
    projected = jnp.sum(sums.astype(F32), axis=0)
    hidden_state = (tokens.astype(F32) + projected).astype(BF16)

    groups = chips * 2
    capacity = max(2, 3 * rows // (2 * groups))
    target_dev = routes[:, 0]
    onehot = (target_dev[:, None] == jnp.arange(groups, dtype=jnp.int32)[None, :]).astype(
        jnp.int32
    ) * masked[:, None]
    before = jnp.cumsum(onehot, axis=0) - onehot
    slot_rank = jnp.sum(before * onehot, axis=1)
    slot_index = jnp.where(masked == 1, target_dev * capacity + slot_rank, groups * capacity)

    cond_other = shifted(cond_weight, "core", 1)
    cond = conditioning_parts(
        core,
        slot_index[None, :],
        hidden_state,
        shifted(hidden_state, "core", 1),
        cond_weight,
        cond_other,
        chips,
        capacity,
    ).reshape(chips, capacity, -1)
    cond = lax.all_to_all(cond, ("zl", "y"), split_axis=0, concat_axis=0, tiled=True)
    conditioning = jnp.sum(cond.astype(F32), axis=0) + cond_bias

    first = lax.axis_index(GRP) * capacity
    own_slots = (
        slot_index[:, None] == first + jnp.arange(capacity, dtype=jnp.int32)[None, :]
    ).astype(F32)
    occupied = jnp.sum(own_slots, axis=0)
    target_rows = jnp.dot(own_slots.T, targets, precision=lax.Precision.HIGHEST)
    noise_rows = jnp.dot(own_slots.T, noise_draws, precision=lax.Precision.HIGHEST)
    steps_float = jnp.dot(own_slots.T, timesteps.astype(F32), precision=lax.Precision.HIGHEST)
    predictions = head_rows(
        conditioning,
        target_rows,
        noise_rows,
        steps_float,
        in_weight,
        mid_weight,
        noise_out_weight,
        head_gain,
    )
    return (hidden_state, predictions * occupied[:, None])


def solution(mesh, sizes=(4, 4, 3, 8, 2)):
    finer = Mesh(mesh.devices.reshape(sizes), ALL)
    in_specs = (
        P(CTX, GRP),
        P(),
        P(None, GRP),
        P(None, GRP),
        P(GRP, None),
        P(),
        P(),
        P(),
        P(),
        P(),
        P(CTX, None),
        P(CTX, None),
        P(CTX, None),
        P(CTX),
        P(CTX, None),
    )
    out_specs = (P(CTX, GRP), P(ALL, None))
    return jax.shard_map(
        shards, mesh=finer, in_specs=in_specs, out_specs=out_specs, check_vma=False
    )
```
